32 devices in a mesh: tm: 16 (over z, x, core), chan: 2 (over y).
Axes of the slice: x: 2, y: 2, z: 4, core: 2. Of those that a mesh axis runs over, the one named last changes fastest.
Arguments:
- series: float32 [64, 8192], P('chan', 'tm'), may hold values from -200 to 200
- tail: float32 [64, 127], P('chan'), may hold values from -200 to 200
- excl: int32 [1], replicated, may hold values from 32 to 128
Outputs:
- profile: float32 [8192], P('tm')
The draws below stay inside these ranges and needn't reach their ends.
All inputs are finite; a program needn't handle non-finite values.
Results may differ from the reference program's by a relative error of at most 0.0003.
Values may be sent and summed in bfloat16 or wider, within the bound.
No kernel may reach another device: no remote copies, remote signals or barrier semaphores. Data moves between devices by JAX's collectives and lax.ppermute only.
A program may use at most 128 MiB of HBM per device.

```python
import math
import jax
import jax.numpy as jnp
from jax import lax

C = 64
M = 128
S_DEV = 512
NT = 8192
N_TM = 16


def common_series(key):
    base = jax.random.fold_in(key, 4242)
    total = NT + M - 1
    factors = 4
    keys = jax.random.split(base, 6)
    rates = jnp.exp(jax.random.uniform(keys[0], (factors,), jnp.float32, jnp.log(0.005), jnp.log(0.1)))
    keepers = 1.0 - rates
    innovation = jax.random.normal(keys[1], (total, factors), jnp.float32)
    drive = jnp.sqrt(1.0 - keepers * keepers)

    def advance(state, entry):
        fresh = keepers * state + drive * entry
        return (fresh, fresh)
    unused, common = lax.scan(advance, jnp.zeros((factors,), jnp.float32), innovation)
    loadings = jax.random.normal(keys[2], (C, factors), jnp.float32)
    noise_level = jax.random.uniform(keys[3], (C, 1), jnp.float32, 0.3, 1.0)
    scales = jnp.exp(jax.random.uniform(keys[4], (C, 1), jnp.float32, 0.0, jnp.log(10.0)))
    noise = jax.random.normal(keys[5], (C, total), jnp.float32)
    values = scales * (jnp.dot(loadings, common.T) + noise_level * noise)
    return jnp.clip(values, -200.0, 200.0)


def draw_series(key, part):
    return common_series(key)[:, :NT]


def draw_tail(key, part):
    return common_series(key)[:, NT:]


def setup_inputs(seed: int = 0) -> dict:
    key_list = jax.random.split(jax.random.key(seed), 4)
    return {
        "series": draw_series(jax.random.fold_in(key_list[3], 71), 0),
        "tail": draw_tail(jax.random.fold_in(key_list[3], 71), 0),
        "excl": jax.random.randint(key_list[2], (1,), M // 4, M + 1).astype(jnp.int32),
    }


EPSILON = 1e-05
CEILING = 4.0

def normalize(extended, count, length, channels):
    starts = jnp.arange(length, dtype=jnp.int32)[:, None] + jnp.arange(count, dtype=jnp.int32)[None, :]
    windows = extended[:, starts]
    center = lax.optimization_barrier(jnp.mean(windows, axis=1, keepdims=True))
    shifted = windows - center
    spread = lax.optimization_barrier(jnp.mean(shifted * shifted, axis=1, keepdims=True))
    factor = lax.rsqrt(spread + EPSILON) * (1.0 / math.sqrt(length * channels))
    return (shifted * factor).astype(jnp.bfloat16)

def reference(series, tail, excl):
    count = S_DEV
    full = jnp.concatenate([series, tail], axis=1)
    total_len = series.shape[1]
    padded = jnp.concatenate([full, jnp.zeros((C, 2 * count), full.dtype)], axis=1)
    limit = excl[0]

    def one_block(block):
        start = block * count
        segment = lax.dynamic_slice_in_dim(padded, start, 3 * count + M - 1, 1)
        zed = normalize(segment, 3 * count, M, C)
        query = zed[:, :, :count].astype(jnp.float32)
        scores = jnp.einsum('cmp,cmq->pq', query, zed.astype(jnp.float32), precision=lax.Precision.HIGHEST)
        rows = start + jnp.arange(count, dtype=jnp.int32)[:, None]
        columns = start + jnp.arange(3 * count, dtype=jnp.int32)[None, :]
        keep = (jnp.abs(rows - columns) >= limit) & (columns < total_len)
        scored = jnp.where(keep, 1.0 - scores, CEILING)
        return (lax.optimization_barrier(jnp.min(scored, axis=1)), lax.optimization_barrier(jnp.min(scored[:, count:2 * count], axis=0)), lax.optimization_barrier(jnp.min(scored[:, 2 * count:], axis=0)))
    row_best, near_cols, far_cols = lax.map(one_block, jnp.arange(N_TM, dtype=jnp.int32))
    filler = jnp.full((2, count), CEILING, row_best.dtype)
    near_cols = jnp.concatenate([filler[:1], near_cols[:-1]], axis=0)
    far_cols = jnp.concatenate([filler, far_cols[:-2]], axis=0)
    return jnp.minimum(row_best, jnp.minimum(near_cols, far_cols)).reshape(-1)
```

```python
import functools
import math

import jax
import jax.numpy as jnp
from jax import lax
from jax.experimental import pallas as pl
from jax.experimental.pallas import tpu as pltpu
from jax.sharding import PartitionSpec as P

EPSILON = 1e-05
CEILING = 4.0
LANES = 128
STEPS = 8


def transposed(source, target):
    channels, length = source.shape
    half = LANES // 2
    value = source[...]
    ahead = pltpu.roll(value, length - half, 1)
    for start in range(0, length, LANES):
        stop = start + LANES
        both = jnp.concatenate([value[:, start:stop], ahead[:, start:stop]], axis=0)
        target[start:stop, :] = both.T


def statistics(samples, sums, moments, mean, scale, count, window, channels):
    half = window // 2
    current = samples
    size = 1
    level = 0
    while size < half:
        rows = -(-(count + half - 2 * size) // 8) * 8
        for start in range(0, rows, 64):
            stop = min(start + 64, rows)
            here = current[start:stop, :]
            there = current[start + size : stop + size, :]
            gap = here - there
            square = gap * gap
            if size > 1:
                old = moments[level % 2]
                square += 2.0 * (old[start:stop, :] + old[start + size : stop + size, :])
            sums[(level + 1) % 2][start:stop, :] = here + there
            moments[(level + 1) % 2][start:stop, :] = square
        level += 1
        current = sums[level % 2]
        size *= 2
    for start in range(0, count, 64):
        here = current[start : start + 64, :]
        there = pltpu.roll(here, LANES // 2, 1)
        gap = here - there
        old = moments[level % 2][start : start + 64, :]
        total = gap * gap + 2.0 * (old + pltpu.roll(old, LANES // 2, 1))
        mean[start : start + 64, :] = (here + there) * (1.0 / window)
        spread = total * (1.0 / (window * window))
        scale[start : start + 64, :] = lax.rsqrt(spread + EPSILON) * (
            1.0 / math.sqrt(window * channels)
        )


def contract(left, right):
    return lax.dot_general(
        left, right, (((1,), (1,)), ((), ())), preferred_element_type=jnp.float32
    )


def body(
    info, near, other, own_out, other_out, samples, means, scales,
    sums_a, sums_b, moments_a, moments_b, zed_a, zed_b, cross, strip, patch,
):
    channels = near.shape[0]
    count = means.shape[1]
    window = 2 * (near.shape[1] - count) // 2
    limit, chan, shift, valid = info[0], info[1], info[2], info[3]
    for index, source in enumerate((near, other)):
        transposed(source, samples.at[index])
        statistics(
            samples.at[index], (sums_a, sums_b), (moments_a, moments_b),
            means.at[index], scales.at[index], count, window, channels,
        )

    def fill(step, zed):
        for index in range(2):
            for start in range(0, count, 16):
                mean = means[index, start : start + 16, :]
                scale = scales[index, start : start + 16, :]
                for inner in range(STEPS):
                    x = samples[index, pl.ds(step * STEPS + (start + inner), 16), :]
                    row = index * count + start
                    zed[row : row + 16, inner * LANES : (inner + 1) * LANES] = (
                        (x - mean) * scale
                    ).astype(jnp.bfloat16)

    def multiply(zed):
        mine = zed[:count, :]
        quarter = count // 4
        cross[...] += contract(zed[count:, :], mine)
        first = pl.multiple_of(chan * quarter, quarter)
        strip[...] += contract(zed[pl.ds(first, quarter), :], mine)
        second = pl.multiple_of(2 * quarter + chan * quarter, quarter)
        patch[...] += contract(zed[pl.ds(second, quarter), :], zed[2 * quarter : count, :])

    cross[...] = jnp.zeros_like(cross)
    strip[...] = jnp.zeros_like(strip)
    patch[...] = jnp.zeros_like(patch)
    fill(0, zed_a)
    rounds = window // 2 // STEPS // 2

    def loop(index, carry):
        fill(2 * index + 1, zed_b)
        multiply(zed_a)
        fill(2 * index + 2, zed_a)
        multiply(zed_b)
        return carry

    lax.fori_loop(0, rounds, loop, 0)

    floor = 1.0 - CEILING
    quarter = count // 4

    def gap(shape, row_start, column_start):
        rows = lax.broadcasted_iota(jnp.int32, shape, 0) + row_start
        columns = lax.broadcasted_iota(jnp.int32, shape, 1) + column_start
        return rows - columns

    def lanes(value):
        best = value[:, :LANES]
        for start in range(LANES, value.shape[1], LANES):
            best = jnp.maximum(best, value[:, start : start + LANES])
        return jnp.max(best.T, axis=0, keepdims=True)

    far = jnp.where(
        (gap(cross.shape, shift * count, 0) >= limit) & (valid > 0), cross[...], floor
    )
    columns = jnp.max(far, axis=0, keepdims=True)
    for index in range(4):
        part = far[index * quarter : (index + 1) * quarter, :]
        other_out[index : index + 1, :] = 1.0 - lanes(part)
    first = jnp.where(jnp.abs(gap(strip.shape, chan * quarter, 0)) >= limit, strip[...], floor)
    columns = jnp.maximum(columns, jnp.max(first, axis=0, keepdims=True))
    second = jnp.where(jnp.abs(gap(patch.shape, chan * quarter, 0)) >= limit, patch[...], floor)
    last = jnp.maximum(columns[:, 2 * quarter :], jnp.max(second, axis=0, keepdims=True))
    pieces = [
        columns[:, :quarter], columns[:, quarter : 2 * quarter],
        last[:, :quarter], last[:, quarter:],
    ]
    lines = [lanes(first), lanes(second)]
    for index in range(4):
        line = jnp.where(chan == index % 2, lines[index // 2], floor)
        own_out[index : index + 1, :] = 1.0 - jnp.maximum(pieces[index], line)


def scores(info, near, other, count):
    channels, length = near.shape
    window = length - count
    wide = STEPS * LANES
    quarter = count // 4
    vmem = pl.BlockSpec(memory_space=pltpu.VMEM)
    return pl.pallas_call(
        body,
        out_shape=[jax.ShapeDtypeStruct((4, quarter), jnp.float32)] * 2,
        in_specs=[pl.BlockSpec(memory_space=pltpu.SMEM), vmem, vmem],
        out_specs=[vmem, vmem],
        scratch_shapes=[
            pltpu.VMEM((2, length, LANES), jnp.float32),
            pltpu.VMEM((2, count, LANES), jnp.float32),
            pltpu.VMEM((2, count, LANES), jnp.float32),
            pltpu.VMEM((length, LANES), jnp.float32),
            pltpu.VMEM((length, LANES), jnp.float32),
            pltpu.VMEM((length, LANES), jnp.float32),
            pltpu.VMEM((length, LANES), jnp.float32),
            pltpu.VMEM((2 * count, wide), jnp.bfloat16),
            pltpu.VMEM((2 * count, wide), jnp.bfloat16),
            pltpu.VMEM((count, count), jnp.float32),
            pltpu.VMEM((quarter, count), jnp.float32),
            pltpu.VMEM((quarter, count // 2), jnp.float32),
        ],
        compiler_params=pltpu.CompilerParams(vmem_limit_bytes=40 << 20),
    )(info, near, other)


def on_device(blocks, chans, series, tail, excl):
    count = series.shape[1]
    width = tail.shape[1]
    block = lax.axis_index("tm")
    chan = lax.axis_index("chan")
    both = ("tm", "chan")
    places = [(b, c) for b in range(blocks) for c in range(chans)]

    def shifted(value, reach):
        pairs = [
            ((b + reach(c)) * chans + c, b * chans + c)
            for b, c in places
            if 0 <= b + reach(c) < blocks
        ]
        return lax.ppermute(value, both, pairs)

    def swapped(value):
        return lax.ppermute(value, "chan", [(c, chans - 1 - c) for c in range(chans)])

    head = shifted(series[:, : width + 1], lambda c: 1)
    head = jnp.where(block == blocks - 1, jnp.pad(tail, ((0, 0), (0, 1))), head)
    extended = jnp.concatenate([series, head], axis=1)
    near = jnp.concatenate([extended, swapped(extended)], axis=0)
    other = shifted(near, lambda c: chans - c)
    shift = chans - chan
    info = jnp.stack([excl[0], chan, shift, (block + shift < blocks).astype(jnp.int32)])
    own, away = scores(info, near, other, count)
    home = shifted(away, lambda c: c - chans)
    best = jnp.minimum(own, jnp.where(block - shift >= 0, home, CEILING))
    return jnp.minimum(best, swapped(best)).reshape(count)


def solution(mesh):
    placed = (P("chan", "tm"), P("chan", None), P())
    run = functools.partial(on_device, mesh.shape["tm"], mesh.shape["chan"])
    return jax.shard_map(run, mesh=mesh, in_specs=placed, out_specs=P("tm"), check_vma=False)
```

```python
import functools
import math

import jax
import jax.numpy as jnp
from jax import lax
from jax.experimental import pallas as pl
from jax.experimental.pallas import tpu as pltpu
from jax.sharding import PartitionSpec as P

EPSILON = 1e-05
CEILING = 4.0
FLOOR = 1.0 - CEILING
LANES = 128
STEPS = (16, 4)


def transposed(value, target):
    length = value.shape[1]
    half = LANES // 2
    ahead = pltpu.roll(value, length - half, 1)
    for start in range(0, length, LANES):
        stop = start + LANES
        both = jnp.concatenate([value[:, start:stop], ahead[:, start:stop]], axis=0)
        target[start:stop, :] = both.T


def statistics(samples, sums, moments, mean, scale, channels):
    count = mean.shape[0]
    window = samples.shape[0] - count
    half = window // 2
    current = samples
    size = 1
    level = 0
    while size < half:
        rows = -(-(count + half - 2 * size) // 8) * 8
        for start in range(0, rows, 64):
            stop = min(start + 64, rows)
            here = current[start:stop, :]
            there = current[start + size : stop + size, :]
            gap = here - there
            square = gap * gap
            if size > 1:
                old = moments[level % 2]
                square += 2.0 * (old[start:stop, :] + old[start + size : stop + size, :])
            sums[(level + 1) % 2][start:stop, :] = here + there
            moments[(level + 1) % 2][start:stop, :] = square
        level += 1
        current = sums[level % 2]
        size *= 2
    for start in range(0, count, 64):
        here = current[start : start + 64, :]
        there = pltpu.roll(here, LANES // 2, 1)
        gap = here - there
        old = moments[level % 2][start : start + 64, :]
        total = gap * gap + 2.0 * (old + pltpu.roll(old, LANES // 2, 1))
        mean[start : start + 64, :] = (here + there) * (1.0 / window)
        spread = total * (1.0 / (window * window))
        scale[start : start + 64, :] = lax.rsqrt(spread + EPSILON) * (
            1.0 / math.sqrt(window * channels)
        )


def contract(left, right):
    return lax.dot_general(
        left, right, (((1,), (1,)), ((), ())), preferred_element_type=jnp.float32
    )


def fill(samples, means, scales, zed, row, step, width):
    for start in range(0, means.shape[0], 16):
        mean = means[start : start + 16, :]
        scale = scales[start : start + 16, :]
        for inner in range(0, width, 2):
            parts = [
                (samples[pl.ds(step + (start + inner + side), 16), :] - mean) * scale
                for side in range(2)
            ]
            zed[row + start : row + start + 16, inner * LANES : (inner + 2) * LANES] = (
                jnp.concatenate(parts, axis=1).astype(jnp.bfloat16)
            )


def streamed(steps, build, multiply):
    width, blocks = steps
    build(0, 0, width)

    def pair(index, carry):
        for slot in range(2):
            build(1 - slot, (2 * index + slot + 1) * width, width)
            multiply(slot, width)
        return carry

    lax.fori_loop(0, blocks // 2, pair, 0)


def gap_of(shape, row_start, column_start):
    rows = lax.broadcasted_iota(jnp.int32, shape, 0) + row_start
    columns = lax.broadcasted_iota(jnp.int32, shape, 1) + column_start
    return rows - columns


def rows_best(value):
    best = value[:, :LANES]
    for start in range(LANES, value.shape[1], LANES):
        best = jnp.maximum(best, value[:, start : start + LANES])
    return jnp.max(best.T, axis=0, keepdims=True)


def own_body(info, near, head, tail, samples, means, scales, sums_a, sums_b, moments_a, moments_b):
    last = jnp.where(info[4] > 0, tail[...], head[...])
    transposed(jnp.concatenate([near[...], last], axis=1), samples)
    statistics(
        samples, (sums_a, sums_b), (moments_a, moments_b), means, scales, near.shape[0]
    )


def cross_body(
    info, samples, means, scales, other, head, tail, away_out, own_out,
    samples_b, means_b, scales_b, sums_a, sums_b, moments_a, moments_b,
    zed_a, zed_b, left, right,
):
    count = means.shape[0]
    half, quarter = count // 2, count // 4
    limit, chan, shift, valid = info[0], info[1], info[2], info[3]
    last = jnp.where(info[5] > 0, tail[...], head[...])
    transposed(jnp.concatenate([other[...], last], axis=1), samples_b)
    statistics(
        samples_b, (sums_a, sums_b), (moments_a, moments_b), means_b, scales_b, other.shape[0]
    )
    zeds = (zed_a, zed_b)
    starts = [
        pl.multiple_of(chan * quarter, quarter),
        pl.multiple_of(half + chan * quarter, quarter),
    ]

    def build(slot, step, width):
        zed = zeds[slot]
        fill(samples, means, scales, zed, 0, step, width)
        fill(samples_b, means_b, scales_b, zed, count, step, width)
        for index, start in enumerate(starts):
            row = 2 * count + index * quarter
            zed[row : row + quarter, :] = zed[pl.ds(start, quarter), :]

    def multiply(slot, width):
        zed = zeds[slot]
        left[...] += contract(zed[count : 2 * count + quarter, :], zed[:half, :])
        right[...] += contract(zed[count : 2 * count + half, :], zed[half:count, :])

    left[...] = jnp.zeros_like(left)
    right[...] = jnp.zeros_like(right)
    streamed(STEPS, build, multiply)

    bests = []
    columns = []
    for index, (block, column) in enumerate(((left, 0), (right, half))):
        value = block[:count, :]
        far = (gap_of(value.shape, shift * count, column) >= limit) & (valid > 0)
        value = jnp.where(far, value, FLOOR)
        bests.append(value)
        columns.append(jnp.max(value, axis=0, keepdims=True))
    far = jnp.maximum(bests[0], bests[1])
    for index in range(4):
        rows = slice(index * quarter, (index + 1) * quarter)
        away_out[index : index + 1, :] = 1.0 - rows_best(far[rows, :])
    lines = []
    for index, start in enumerate(starts):
        rows = slice(count + index * quarter, count + (index + 1) * quarter)
        best = None
        for block, column in ((left, 0), (right, half))[index:]:
            value = block[rows, :]
            value = jnp.where(jnp.abs(gap_of(value.shape, start, column)) >= limit, value, FLOOR)
            side = column // half
            columns[side] = jnp.maximum(columns[side], jnp.max(value, axis=0, keepdims=True))
            best = value if best is None else jnp.maximum(best, value)
        lines.append(rows_best(best))
    for index in range(4):
        place = slice((index % 2) * quarter, (index % 2 + 1) * quarter)
        line = jnp.where(chan == index % 2, lines[index // 2], FLOOR)
        own_out[index : index + 1, :] = 1.0 - jnp.maximum(columns[index // 2][:, place], line)


SMEM = pl.BlockSpec(memory_space=pltpu.SMEM)
VMEM = pl.BlockSpec(memory_space=pltpu.VMEM)


def sized(*shape, dtype=jnp.float32):
    return jax.ShapeDtypeStruct(shape, dtype)


def prepare(info, near, head, tail):
    channels, count = near.shape
    length = count + head.shape[1]
    return pl.pallas_call(
        own_body,
        out_shape=[sized(length, LANES), sized(count, LANES), sized(count, LANES)],
        in_specs=[SMEM, VMEM, VMEM, VMEM],
        out_specs=[VMEM] * 3,
        scratch_shapes=[pltpu.VMEM((length, LANES), jnp.float32)] * 4,
        compiler_params=pltpu.CompilerParams(vmem_limit_bytes=8 << 20),
        cost_estimate=pl.CostEstimate(flops=4_000_000, bytes_accessed=1 << 21, transcendentals=0),
    )(info, near, head, tail)


def crossed(info, own, other, head, tail):
    channels, count = other.shape
    length = count + head.shape[1]
    quarter = count // 4
    wide = STEPS[0] * LANES
    flops = 2 * count * count * channels * (length - count)
    return pl.pallas_call(
        cross_body,
        out_shape=[sized(4, quarter)] * 2,
        in_specs=[SMEM] + [VMEM] * 6,
        out_specs=[VMEM] * 2,
        scratch_shapes=[
            pltpu.VMEM((length, LANES), jnp.float32),
            pltpu.VMEM((count, LANES), jnp.float32),
            pltpu.VMEM((count, LANES), jnp.float32),
            *[pltpu.VMEM((length, LANES), jnp.float32)] * 4,
            *[pltpu.VMEM((2 * count + count // 2, wide), jnp.bfloat16)] * 2,
            pltpu.VMEM((count + quarter, count // 2), jnp.float32),
            pltpu.VMEM((count + count // 2, count // 2), jnp.float32),
        ],
        compiler_params=pltpu.CompilerParams(vmem_limit_bytes=32 << 20),
        cost_estimate=pl.CostEstimate(flops=flops, bytes_accessed=1 << 21, transcendentals=0),
    )(info, *own, other, head, tail)


def on_device(blocks, chans, series, tail, excl):
    count = series.shape[1]
    window = tail.shape[1] + 1
    block = lax.axis_index("tm")
    chan = lax.axis_index("chan")
    axes = ("tm", "chan")
    places = [(b, c) for b in range(blocks) for c in range(chans)]

    def shifted(value, reach):
        pairs = [
            ((b + reach(c)) * chans + c, b * chans + c)
            for b, c in places
            if 0 <= b + reach(c) < blocks
        ]
        return lax.ppermute(value, axes, pairs)

    def swapped(value):
        return lax.ppermute(value, "chan", [(c, chans - 1 - c) for c in range(chans)])

    shift = chans - chan
    flags = [block + shift < blocks, block == blocks - 1, block + shift == blocks - 1]
    info = jnp.stack([excl[0], chan, shift] + [flag.astype(jnp.int32) for flag in flags])
    spare = jnp.zeros((series.shape[0], 1), series.dtype)
    padded = jnp.concatenate([series, tail, spare], axis=1)
    partner = swapped(padded)
    near = jnp.concatenate([padded[:, :count], partner[:, :count]], axis=0)
    ending = jnp.concatenate([padded[:, count:], partner[:, count:]], axis=0)
    with jax.named_scope("block"):
        other = shifted(near, lambda c: chans - c)
    with jax.named_scope("next_head"):
        head = shifted(near[:, :window], lambda c: 1)
    with jax.named_scope("far_head"):
        other_head = shifted(near[:, :window], lambda c: chans + 1 - c)
    own = prepare(info, near, head, ending)
    away, best = crossed(info, own, other, other_head, ending)
    home = shifted(away, lambda c: c - chans)
    best = jnp.minimum(best, jnp.where(block - shift >= 0, home, CEILING))
    return jnp.minimum(best, swapped(best)).reshape(count)


def solution(mesh):
    placed = (P("chan", "tm"), P("chan", None), P())
    run = functools.partial(on_device, mesh.shape["tm"], mesh.shape["chan"])
    return jax.shard_map(run, mesh=mesh, in_specs=placed, out_specs=P("tm"), check_vma=False)
```

```python
import functools
import math

import jax
import jax.numpy as jnp
from jax import lax
from jax.experimental import pallas as pl
from jax.experimental.pallas import tpu as pltpu
from jax.sharding import PartitionSpec as P


EPSILON = 1e-05
CEILING = 4.0
FLOOR = 1.0 - CEILING
LANES = 128
WIDTH = 16


def transposed(value, target):
    length = value.shape[1]
    half = LANES // 2
    ahead = pltpu.roll(value, length - half, 1)
    for start in range(0, length, LANES):
        stop = start + LANES
        both = jnp.concatenate([value[:, start:stop], ahead[:, start:stop]], axis=0)
        target[start:stop, :] = both.T


def statistics(samples, sums, moments, mean, scale, channels):
    count = mean.shape[0]
    window = samples.shape[0] - count
    half = window // 2
    current = samples
    size = 1
    level = 0
    while size < half:
        rows = -(-(count + half - 2 * size) // 8) * 8
        for start in range(0, rows, 64):
            stop = min(start + 64, rows)
            here = current[start:stop, :]
            there = current[start + size : stop + size, :]
            gap = here - there
            square = gap * gap
            if size > 1:
                old = moments[level % 2]
                square += 2.0 * (old[start:stop, :] + old[start + size : stop + size, :])
            sums[(level + 1) % 2][start:stop, :] = here + there
            moments[(level + 1) % 2][start:stop, :] = square
        level += 1
        current = sums[level % 2]
        size *= 2
    for start in range(0, count, 64):
        here = current[start : start + 64, :]
        there = pltpu.roll(here, LANES // 2, 1)
        gap = here - there
        old = moments[level % 2][start : start + 64, :]
        total = gap * gap + 2.0 * (old + pltpu.roll(old, LANES // 2, 1))
        mean[start : start + 64, :] = (here + there) * (1.0 / window)
        spread = total * (1.0 / (window * window))
        scale[start : start + 64, :] = lax.rsqrt(spread + EPSILON) * (
            1.0 / math.sqrt(window * channels)
        )


def contract(left, right):
    return lax.dot_general(
        left, right, (((1,), (1,)), ((), ())), preferred_element_type=jnp.float32
    )


def fill(samples, means, scales, zed, step, base):
    for start in range(0, means.shape[0], 16):
        mean = means[start : start + 16, :]
        scale = scales[start : start + 16, :]
        for inner in range(0, WIDTH, 2):
            parts = [
                (samples[pl.ds(step + (start + inner + side), 16), :] - mean) * scale
                for side in range(2)
            ]
            zed[start : start + 16, pl.ds(base + inner * LANES, 2 * LANES)] = (
                jnp.concatenate(parts, axis=1).astype(jnp.bfloat16)
            )


def block_of(index):
    return pl.multiple_of(index * (WIDTH * LANES), WIDTH * LANES)


def gap_of(shape, row_start, column_start):
    rows = lax.broadcasted_iota(jnp.int32, shape, 0) + row_start
    columns = lax.broadcasted_iota(jnp.int32, shape, 1) + column_start
    return rows - columns


def rows_best(value):
    best = value[:, :LANES]
    for start in range(LANES, value.shape[1], LANES):
        best = jnp.maximum(best, value[:, start : start + LANES])
    return jnp.max(best.T, axis=0, keepdims=True)


def own_body(
    info, near, head, tail, zed_out,
    samples, means, scales, sums_a, sums_b, moments_a, moments_b,
):
    last = jnp.where(info[4] > 0, tail[...], head[...])
    transposed(jnp.concatenate([near[...], last], axis=1), samples)
    statistics(
        samples, (sums_a, sums_b), (moments_a, moments_b), means, scales, near.shape[0]
    )

    def build(index, carry):
        fill(samples, means, scales, zed_out, index * WIDTH, block_of(index))
        return carry

    lax.fori_loop(0, zed_out.shape[1] // (WIDTH * LANES), build, 0)


def cross_body(
    info, mine, other, head, tail, away_out, part_out,
    samples, means, scales, sums_a, sums_b, moments_a, moments_b, zed_a, zed_b, cross,
):
    count = means.shape[0]
    quarter = count // 4
    limit, shift, valid = info[0], info[2], info[3]
    last = jnp.where(info[5] > 0, tail[...], head[...])
    transposed(jnp.concatenate([other[...], last], axis=1), samples)
    statistics(
        samples, (sums_a, sums_b), (moments_a, moments_b), means, scales, other.shape[0]
    )
    zeds = (zed_a, zed_b)
    cross[...] = jnp.zeros_like(cross)
    fill(samples, means, scales, zed_a, 0, 0)

    def pair(index, carry):
        for slot in range(2):
            block = 2 * index + slot
            cross[...] += contract(
                zeds[slot][...], mine[:, pl.ds(block_of(block), WIDTH * LANES)]
            )
            fill(samples, means, scales, zeds[1 - slot], (block + 1) * WIDTH, 0)
        return carry

    lax.fori_loop(0, mine.shape[1] // (2 * WIDTH * LANES), pair, 0)
    far = jnp.where(
        (gap_of(cross.shape, shift * count, 0) >= limit) & (valid > 0), cross[...], FLOOR
    )
    columns = jnp.max(far, axis=0, keepdims=True)
    for index in range(4):
        rows = slice(index * quarter, (index + 1) * quarter)
        away_out[index : index + 1, :] = 1.0 - rows_best(far[rows, :])
        part_out[index : index + 1, :] = columns[:, rows]


def pair_body(info, mine, part, own_out, stage_a, stage_b, pair):
    count = mine.shape[0]
    quarter = count // 4
    limit, chan = info[0], info[1]
    stages = (stage_a, stage_b)
    starts = [
        pl.multiple_of(chan * quarter, quarter),
        pl.multiple_of(2 * quarter + chan * quarter, quarter),
    ]
    pair[...] = jnp.zeros_like(pair)

    def step(index, carry):
        for slot in range(2):
            lanes = pl.ds(block_of(2 * index + slot), WIDTH * LANES)
            for place, start in enumerate(starts):
                stages[slot][place * quarter : (place + 1) * quarter, :] = mine[
                    pl.ds(start, quarter), lanes
                ]
            pair[...] += contract(mine[:, lanes], stages[slot][...])
        return carry

    lax.fori_loop(0, mine.shape[1] // (2 * WIDTH * LANES), step, 0)
    near = []
    for index, start in enumerate(starts):
        value = pair[:, index * quarter : (index + 1) * quarter]
        near.append(jnp.where(jnp.abs(gap_of(value.shape, 0, start)) >= limit, value, FLOOR))
    lines = [jnp.max(value, axis=0, keepdims=True) for value in near]
    both = jnp.maximum(near[0], near[1])
    for index in range(4):
        best = rows_best(both[index * quarter : (index + 1) * quarter, :])
        best = jnp.maximum(best, part[index : index + 1, :])
        line = jnp.where(chan == index % 2, lines[index // 2], FLOOR)
        own_out[index : index + 1, :] = 1.0 - jnp.maximum(best, line)


SMEM = pl.BlockSpec(memory_space=pltpu.SMEM)
VMEM = pl.BlockSpec(memory_space=pltpu.VMEM)


def sized(*shape, dtype=jnp.float32):
    return jax.ShapeDtypeStruct(shape, dtype)


def working(count, length):
    long, short = pltpu.VMEM((length, LANES), jnp.float32), pltpu.VMEM((count, LANES), jnp.float32)
    return [long, short, short, long, long, long, long]


def settings(flops):
    return dict(
        compiler_params=pltpu.CompilerParams(vmem_limit_bytes=16 << 20),
        cost_estimate=pl.CostEstimate(flops=flops, bytes_accessed=1 << 21, transcendentals=0),
    )


def prepare(info, near, head, tail):
    channels, count = near.shape
    window = head.shape[1]
    return pl.pallas_call(
        own_body,
        out_shape=sized(count, channels * window, dtype=jnp.bfloat16),
        in_specs=[SMEM, VMEM, VMEM, VMEM],
        out_specs=VMEM,
        scratch_shapes=working(count, count + window),
        **settings(count * channels * window * 100),
    )(info, near, head, tail)


def crossed(info, mine, other, head, tail):
    channels, count = other.shape
    window = head.shape[1]
    return pl.pallas_call(
        cross_body,
        out_shape=[sized(4, count // 4)] * 2,
        in_specs=[SMEM] + [VMEM] * 4,
        out_specs=[VMEM] * 2,
        scratch_shapes=[
            *working(count, count + window),
            *[pltpu.VMEM((count, WIDTH * LANES), jnp.bfloat16)] * 2,
            pltpu.VMEM((count, count), jnp.float32),
        ],
        **settings(2 * count * count * channels * window),
    )(info, mine, other, head, tail)


def paired(info, mine, part):
    count, depth = mine.shape
    return pl.pallas_call(
        pair_body,
        out_shape=sized(4, count // 4),
        in_specs=[SMEM] + [VMEM] * 2,
        out_specs=VMEM,
        scratch_shapes=[
            *[pltpu.VMEM((count // 2, WIDTH * LANES), jnp.bfloat16)] * 2,
            pltpu.VMEM((count, count // 2), jnp.float32),
        ],
        **settings(count * count * depth),
    )(info, mine, part)


def on_device(blocks, chans, series, tail, excl):
    return profile(blocks, chans, series, tail, excl)


def profile(blocks, chans, series, tail, excl):
    count = series.shape[1]
    window = tail.shape[1] + 1
    block = lax.axis_index("tm")
    chan = lax.axis_index("chan")
    axes = ("tm", "chan")
    places = [(b, c) for b in range(blocks) for c in range(chans)]

    def shifted(value, reach):
        pairs = [
            ((b + reach(c)) * chans + c, b * chans + c)
            for b, c in places
            if 0 <= b + reach(c) < blocks
        ]
        return lax.ppermute(value, axes, pairs)

    def swapped(value):
        return lax.ppermute(value, "chan", [(c, chans - 1 - c) for c in range(chans)])

    shift = chans - chan
    flags = [block + shift < blocks, block == blocks - 1, block + shift == blocks - 1]
    info = jnp.stack([excl[0], chan, shift] + [flag.astype(jnp.int32) for flag in flags])
    spare = jnp.zeros((series.shape[0], 1), series.dtype)
    padded = lax.optimization_barrier(jnp.concatenate([series, tail, spare], axis=1))
    partner = swapped(padded)
    near = jnp.concatenate([padded[:, :count], partner[:, :count]], axis=0)
    ending = jnp.concatenate([padded[:, count:], partner[:, count:]], axis=0)
    other = shifted(near, lambda c: chans - c)
    head = shifted(near[:, :window], lambda c: 1)
    other_head = shifted(near[:, :window], lambda c: chans + 1 - c)
    mine = prepare(info, near, head, ending)
    away, part = crossed(info, mine, other, other_head, ending)
    home = shifted(away, lambda c: c - chans)
    best = paired(info, mine, part)
    best = jnp.minimum(best, jnp.where(block - shift >= 0, home, CEILING))
    return jnp.minimum(best, swapped(best)).reshape(count)


def solution(mesh):
    placed = (P("chan", "tm"), P("chan", None), P())
    run = functools.partial(on_device, mesh.shape["tm"], mesh.shape["chan"])
    return jax.shard_map(run, mesh=mesh, in_specs=placed, out_specs=P("tm"), check_vma=False)
```

```python
import functools
import math

import jax
import jax.numpy as jnp
from jax import lax
from jax.experimental import pallas as pl
from jax.experimental.pallas import tpu as pltpu
from jax.sharding import PartitionSpec as P


EPSILON = 1e-05
CEILING = 4.0
FLOOR = 1.0 - CEILING
LANES = 128
WIDTH = 16


def transposed(value, target):
    length = value.shape[1]
    half = LANES // 2
    ahead = pltpu.roll(value, length - half, 1)
    for start in range(0, length, LANES):
        stop = start + LANES
        both = jnp.concatenate([value[:, start:stop], ahead[:, start:stop]], axis=0)
        target[start:stop, :] = both.T


def statistics(samples, sums, moments, mean, scale, channels):
    count = mean.shape[0]
    window = samples.shape[0] - count
    half = window // 2
    current = samples
    size = 1
    level = 0
    while size < half:
        rows = -(-(count + half - 2 * size) // 8) * 8
        for start in range(0, rows, 64):
            stop = min(start + 64, rows)
            here = current[start:stop, :]
            there = current[start + size : stop + size, :]
            gap = here - there
            square = gap * gap
            if size > 1:
                old = moments[level % 2]
                square += 2.0 * (old[start:stop, :] + old[start + size : stop + size, :])
            sums[(level + 1) % 2][start:stop, :] = here + there
            moments[(level + 1) % 2][start:stop, :] = square
        level += 1
        current = sums[level % 2]
        size *= 2
    for start in range(0, count, 64):
        here = current[start : start + 64, :]
        there = pltpu.roll(here, LANES // 2, 1)
        gap = here - there
        old = moments[level % 2][start : start + 64, :]
        total = gap * gap + 2.0 * (old + pltpu.roll(old, LANES // 2, 1))
        mean[start : start + 64, :] = (here + there) * (1.0 / window)
        spread = total * (1.0 / (window * window))
        scale[start : start + 64, :] = lax.rsqrt(spread + EPSILON) * (
            1.0 / math.sqrt(window * channels)
        )


def contract(left, right):
    return lax.dot_general(
        left, right, (((1,), (1,)), ((), ())), preferred_element_type=jnp.float32
    )


def fill(samples, means, scales, zed, step, base):
    for start in range(0, means.shape[0], 16):
        mean = means[start : start + 16, :]
        scale = scales[start : start + 16, :]
        for inner in range(0, WIDTH, 2):
            parts = [
                (samples[pl.ds(step + (start + inner + side), 16), :] - mean) * scale
                for side in range(2)
            ]
            zed[start : start + 16, pl.ds(base + inner * LANES, 2 * LANES)] = (
                jnp.concatenate(parts, axis=1).astype(jnp.bfloat16)
            )


def block_of(index):
    return pl.multiple_of(index * (WIDTH * LANES), WIDTH * LANES)


def gap_of(shape, row_start, column_start):
    rows = lax.broadcasted_iota(jnp.int32, shape, 0) + row_start
    columns = lax.broadcasted_iota(jnp.int32, shape, 1) + column_start
    return rows - columns


def rows_best(value):
    best = value[:, :LANES]
    for start in range(LANES, value.shape[1], LANES):
        best = jnp.maximum(best, value[:, start : start + LANES])
    return jnp.max(best.T, axis=0, keepdims=True)


def own_body(
    info, near, head, tail, zed_out,
    samples, means, scales, sums_a, sums_b, moments_a, moments_b,
):
    last = jnp.where(info[4] > 0, tail[...], head[...])
    transposed(jnp.concatenate([near[...], last], axis=1), samples)
    statistics(
        samples, (sums_a, sums_b), (moments_a, moments_b), means, scales, near.shape[0]
    )

    def build(index, carry):
        fill(samples, means, scales, zed_out, index * WIDTH, block_of(index))
        return carry

    lax.fori_loop(0, zed_out.shape[1] // (WIDTH * LANES), build, 0)


def staged(mine, stage, base, chan):
    quarter = mine.shape[0] // 4
    for place in range(2):
        start = pl.multiple_of((2 * place + chan) * quarter, quarter)
        stage[place * quarter : (place + 1) * quarter, :] = mine[
            pl.ds(start, quarter), pl.ds(base, WIDTH * LANES)
        ]


def cross_body(
    info, mine, other, head, tail, away_out, part_out, pair_out,
    samples, means, scales, sums_a, sums_b, moments_a, moments_b, zed_a, zed_b, cross,
    stage_a, stage_b,
):
    count = means.shape[0]
    quarter = count // 4
    limit, shift, valid = info[0], info[2], info[3]
    for block, stage in enumerate((stage_a, stage_b)):
        staged(mine, stage, block_of(block), info[1])
        value = contract(mine[:, pl.ds(block_of(block), WIDTH * LANES)], stage[...])
        pair_out[...] = pair_out[...] + value if block else value
    last = jnp.where(info[5] > 0, tail[...], head[...])
    transposed(jnp.concatenate([other[...], last], axis=1), samples)
    statistics(
        samples, (sums_a, sums_b), (moments_a, moments_b), means, scales, other.shape[0]
    )
    zeds = (zed_a, zed_b)
    cross[...] = jnp.zeros_like(cross)
    fill(samples, means, scales, zed_a, 0, 0)

    def pair(index, carry):
        for slot in range(2):
            block = 2 * index + slot
            cross[...] += contract(
                zeds[slot][...], mine[:, pl.ds(block_of(block), WIDTH * LANES)]
            )
            fill(samples, means, scales, zeds[1 - slot], (block + 1) * WIDTH, 0)
        return carry

    lax.fori_loop(0, mine.shape[1] // (2 * WIDTH * LANES), pair, 0)
    far = jnp.where(
        (gap_of(cross.shape, shift * count, 0) >= limit) & (valid > 0), cross[...], FLOOR
    )
    columns = jnp.max(far, axis=0, keepdims=True)
    for index in range(4):
        rows = slice(index * quarter, (index + 1) * quarter)
        away_out[index : index + 1, :] = 1.0 - rows_best(far[rows, :])
        part_out[index : index + 1, :] = columns[:, rows]


def pair_body(info, mine, part, partial, own_out, stage_a, stage_b, pair):
    count = mine.shape[0]
    quarter = count // 4
    limit, chan = info[0], info[1]
    stages = (stage_a, stage_b)
    starts = [
        pl.multiple_of(chan * quarter, quarter),
        pl.multiple_of(2 * quarter + chan * quarter, quarter),
    ]
    blocks = mine.shape[1] // (WIDTH * LANES)
    for slot in range(2):
        base = block_of(blocks - 2 + slot)
        staged(mine, stages[slot], base, chan)
        value = contract(mine[:, pl.ds(base, WIDTH * LANES)], stages[slot][...])
        pair[...] = (pair if slot else partial)[...] + value
    near = []
    for index, start in enumerate(starts):
        value = pair[:, index * quarter : (index + 1) * quarter]
        near.append(jnp.where(jnp.abs(gap_of(value.shape, 0, start)) >= limit, value, FLOOR))
    lines = [jnp.max(value, axis=0, keepdims=True) for value in near]
    both = jnp.maximum(near[0], near[1])
    for index in range(4):
        best = rows_best(both[index * quarter : (index + 1) * quarter, :])
        best = jnp.maximum(best, part[index : index + 1, :])
        line = jnp.where(chan == index % 2, lines[index // 2], FLOOR)
        own_out[index : index + 1, :] = 1.0 - jnp.maximum(best, line)


SMEM = pl.BlockSpec(memory_space=pltpu.SMEM)
VMEM = pl.BlockSpec(memory_space=pltpu.VMEM)


def sized(*shape, dtype=jnp.float32):
    return jax.ShapeDtypeStruct(shape, dtype)


def working(count, length):
    long, short = pltpu.VMEM((length, LANES), jnp.float32), pltpu.VMEM((count, LANES), jnp.float32)
    return [long, short, short, long, long, long, long]


def settings(flops):
    return dict(
        compiler_params=pltpu.CompilerParams(vmem_limit_bytes=16 << 20),
        cost_estimate=pl.CostEstimate(flops=flops, bytes_accessed=1 << 21, transcendentals=0),
    )


def prepare(info, near, head, tail):
    channels, count = near.shape
    window = head.shape[1]
    return pl.pallas_call(
        own_body,
        out_shape=sized(count, channels * window, dtype=jnp.bfloat16),
        in_specs=[SMEM, VMEM, VMEM, VMEM],
        out_specs=VMEM,
        scratch_shapes=working(count, count + window),
        **settings(count * channels * window * 100),
    )(info, near, head, tail)


def crossed(info, mine, other, head, tail):
    channels, count = other.shape
    window = head.shape[1]
    return pl.pallas_call(
        cross_body,
        out_shape=[sized(4, count // 4)] * 2 + [sized(count, count // 2)],
        in_specs=[SMEM] + [VMEM] * 4,
        out_specs=[VMEM] * 3,
        scratch_shapes=[
            *working(count, count + window),
            *[pltpu.VMEM((count, WIDTH * LANES), jnp.bfloat16)] * 2,
            pltpu.VMEM((count, count), jnp.float32),
            *[pltpu.VMEM((count // 2, WIDTH * LANES), jnp.bfloat16)] * 2,
        ],
        **settings(2 * count * count * channels * window),
    )(info, mine, other, head, tail)


def paired(info, mine, part, partial):
    count, depth = mine.shape
    return pl.pallas_call(
        pair_body,
        out_shape=sized(4, count // 4),
        in_specs=[SMEM] + [VMEM] * 3,
        out_specs=VMEM,
        scratch_shapes=[
            *[pltpu.VMEM((count // 2, WIDTH * LANES), jnp.bfloat16)] * 2,
            pltpu.VMEM((count, count // 2), jnp.float32),
        ],
        **settings(count * count * depth),
    )(info, mine, part, partial)


def on_device(blocks, chans, series, tail, excl):
    return profile(blocks, chans, series, tail, excl)


def profile(blocks, chans, series, tail, excl):
    count = series.shape[1]
    window = tail.shape[1] + 1
    block = lax.axis_index("tm")
    chan = lax.axis_index("chan")
    axes = ("tm", "chan")
    places = [(b, c) for b in range(blocks) for c in range(chans)]

    def shifted(value, reach):
        pairs = [
            ((b + reach(c)) * chans + c, b * chans + c)
            for b, c in places
            if 0 <= b + reach(c) < blocks
        ]
        return lax.ppermute(value, axes, pairs)

    def swapped(value):
        return lax.ppermute(value, "chan", [(c, chans - 1 - c) for c in range(chans)])

    shift = chans - chan
    flags = [block + shift < blocks, block == blocks - 1, block + shift == blocks - 1]
    info = jnp.stack([excl[0], chan, shift] + [flag.astype(jnp.int32) for flag in flags])
    spare = jnp.zeros((series.shape[0], 1), series.dtype)
    partner = swapped(series)
    ends = [(b, c) for b, c in places if b >= blocks - 1 - chans]
    pairs = [(b * chans + c, b * chans + chans - 1 - c) for b, c in ends]
    partner_tail = lax.ppermute(tail, axes, pairs)
    padded = lax.optimization_barrier(jnp.concatenate([series, tail, spare], axis=1))
    near = jnp.concatenate([padded[:, :count], partner], axis=0)
    partner_tail = jnp.concatenate([partner_tail, spare], axis=1)
    ending = jnp.concatenate([padded[:, count:], partner_tail], axis=0)
    other = shifted(near, lambda c: chans - c)
    head = shifted(near[:, :window], lambda c: 1)
    other_head = shifted(near[:, :window], lambda c: chans + 1 - c)
    mine = prepare(info, near, head, ending)
    away, part, partial = crossed(info, mine, other, other_head, ending)
    home = shifted(away, lambda c: c - chans)
    best = paired(info, mine, part, partial)
    best = jnp.minimum(best, jnp.where(block - shift >= 0, home, CEILING))
    return jnp.minimum(best, swapped(best)).reshape(count)


def solution(mesh):
    placed = (P("chan", "tm"), P("chan", None), P())
    run = functools.partial(on_device, mesh.shape["tm"], mesh.shape["chan"])
    return jax.shard_map(run, mesh=mesh, in_specs=placed, out_specs=P("tm"), check_vma=False)
```

```python
import functools
import math

import jax
import jax.numpy as jnp
from jax import lax
from jax.experimental import pallas as pl
from jax.experimental.pallas import tpu as pltpu
from jax.sharding import PartitionSpec as P


EPSILON = 1e-05
CEILING = 4.0
FLOOR = 1.0 - CEILING
LANES = 128
WIDTH = 16


def transposed(value, target):
    length = value.shape[1]
    half = LANES // 2
    ahead = pltpu.roll(value, length - half, 1)
    for start in range(0, length, LANES):
        stop = start + LANES
        both = jnp.concatenate([value[:, start:stop], ahead[:, start:stop]], axis=0)
        target[start:stop, :] = both.T


def statistics(value, sums, moments, mean, scale):
    channels = value.shape[0]
    count = mean.shape[0]
    half = count // 2
    window = value.shape[1] - count
    for start in range(0, half + window, LANES):
        stop = start + LANES
        both = jnp.concatenate([value[:, start:stop], value[:, half + start : half + stop]], axis=0)
        sums[0][start:stop, :] = both.T
    size = 1
    level = 0
    while size < window:
        rows = -(-(half + window - 2 * size) // 8) * 8
        old, new = sums[level % 2], sums[(level + 1) % 2]
        for start in range(0, rows, 64):
            stop = min(start + 64, rows)
            here = old[start:stop, :]
            there = old[start + size : stop + size, :]
            gap = here - there
            square = gap * gap
            if size > 1:
                past = moments[level % 2]
                square += 2.0 * (past[start:stop, :] + past[start + size : stop + size, :])
            new[start:stop, :] = here + there
            moments[(level + 1) % 2][start:stop, :] = square
        level += 1
        size *= 2
    lower = lax.broadcasted_iota(jnp.int32, (64, LANES), 1) < LANES // 2
    for start in range(0, half, 64):
        rows = slice(start, start + 64)
        center = sums[level % 2][rows, :] * (1.0 / window)
        spread = moments[level % 2][rows, :] * (1.0 / (window * window))
        factor = lax.rsqrt(spread + EPSILON) * (1.0 / math.sqrt(window * channels))
        for target, part in ((mean, center), (scale, factor)):
            other = pltpu.roll(part, LANES // 2, 1)
            target[rows, :] = jnp.where(lower, part, other)
            target[half + start : half + start + 64, :] = jnp.where(lower, other, part)


def contract(left, right):
    return lax.dot_general(
        left, right, (((1,), (1,)), ((), ())), preferred_element_type=jnp.float32
    )


def fill(samples, means, scales, zed, step, base):
    for start in range(0, means.shape[0], 16):
        mean = means[start : start + 16, :]
        scale = scales[start : start + 16, :]
        for inner in range(0, WIDTH, 2):
            parts = [
                (samples[pl.ds(step + (start + inner + side), 16), :] - mean) * scale
                for side in range(2)
            ]
            zed[start : start + 16, pl.ds(base + inner * LANES, 2 * LANES)] = (
                jnp.concatenate(parts, axis=1).astype(jnp.bfloat16)
            )


def block_of(index):
    return pl.multiple_of(index * (WIDTH * LANES), WIDTH * LANES)


def gap_of(shape, row_start, column_start):
    rows = lax.broadcasted_iota(jnp.int32, shape, 0) + row_start
    columns = lax.broadcasted_iota(jnp.int32, shape, 1) + column_start
    return rows - columns


def rows_best(value):
    best = value[:, :LANES]
    for start in range(LANES, value.shape[1], LANES):
        best = jnp.maximum(best, value[:, start : start + LANES])
    return jnp.max(best.T, axis=0, keepdims=True)


def own_body(
    info, near, head, tail, zed_out,
    samples, means, scales, sums_a, sums_b, moments_a, moments_b,
):
    last = jnp.where(info[4] > 0, tail[...], head[...])
    value = jnp.concatenate([near[...], last], axis=1)
    transposed(value, samples)
    statistics(value, (sums_a, sums_b), (moments_a, moments_b), means, scales)

    def build(index, carry):
        fill(samples, means, scales, zed_out, index * WIDTH, block_of(index))
        return carry

    lax.fori_loop(0, zed_out.shape[1] // (WIDTH * LANES), build, 0)


def staged(mine, stage, base, chan):
    quarter = mine.shape[0] // 4
    for place in range(2):
        start = pl.multiple_of((2 * place + chan) * quarter, quarter)
        stage[place * quarter : (place + 1) * quarter, :] = mine[
            pl.ds(start, quarter), pl.ds(base, WIDTH * LANES)
        ]


def cross_body(
    info, mine, other, head, tail, away_out, part_out, pair_out,
    samples, means, scales, sums_a, sums_b, moments_a, moments_b, zed_a, zed_b, cross,
    stage_a, stage_b,
):
    count = means.shape[0]
    quarter = count // 4
    limit, shift, valid = info[0], info[2], info[3]
    last = jnp.where(info[5] > 0, tail[...], head[...])
    value = jnp.concatenate([other[...], last], axis=1)
    transposed(value, samples)
    staged(mine, stage_a, block_of(0), info[1])
    product = contract(mine[:, pl.ds(block_of(0), WIDTH * LANES)], stage_a[...])
    pair_out[...] = product
    statistics(value, (sums_a, sums_b), (moments_a, moments_b), means, scales)
    staged(mine, stage_b, block_of(1), info[1])
    product = contract(mine[:, pl.ds(block_of(1), WIDTH * LANES)], stage_b[...])
    pair_out[...] = pair_out[...] + product
    zeds = (zed_a, zed_b)
    cross[...] = jnp.zeros_like(cross)
    fill(samples, means, scales, zed_a, 0, 0)

    def pair(index, carry):
        for slot in range(2):
            block = 2 * index + slot
            cross[...] += contract(
                zeds[slot][...], mine[:, pl.ds(block_of(block), WIDTH * LANES)]
            )
            fill(samples, means, scales, zeds[1 - slot], (block + 1) * WIDTH, 0)
        return carry

    lax.fori_loop(0, mine.shape[1] // (2 * WIDTH * LANES), pair, 0, unroll=True)
    far = jnp.where(
        (gap_of(cross.shape, shift * count, 0) >= limit) & (valid > 0), cross[...], FLOOR
    )
    columns = jnp.max(far, axis=0, keepdims=True)
    for index in range(4):
        rows = slice(index * quarter, (index + 1) * quarter)
        away_out[index : index + 1, :] = 1.0 - rows_best(far[rows, :])
        part_out[index : index + 1, :] = columns[:, rows]


def pair_body(info, mine, part, partial, own_out, stage_a, stage_b, pair):
    count = mine.shape[0]
    quarter = count // 4
    limit, chan = info[0], info[1]
    stages = (stage_a, stage_b)
    starts = [
        pl.multiple_of(chan * quarter, quarter),
        pl.multiple_of(2 * quarter + chan * quarter, quarter),
    ]
    blocks = mine.shape[1] // (WIDTH * LANES)
    for slot in range(2):
        base = block_of(blocks - 2 + slot)
        staged(mine, stages[slot], base, chan)
        value = contract(mine[:, pl.ds(base, WIDTH * LANES)], stages[slot][...])
        pair[...] = (pair if slot else partial)[...] + value
    near = []
    for index, start in enumerate(starts):
        value = pair[:, index * quarter : (index + 1) * quarter]
        near.append(jnp.where(jnp.abs(gap_of(value.shape, 0, start)) >= limit, value, FLOOR))
    lines = [jnp.max(value, axis=0, keepdims=True) for value in near]
    both = jnp.maximum(near[0], near[1])
    for index in range(4):
        best = rows_best(both[index * quarter : (index + 1) * quarter, :])
        best = jnp.maximum(best, part[index : index + 1, :])
        line = jnp.where(chan == index % 2, lines[index // 2], FLOOR)
        own_out[index : index + 1, :] = 1.0 - jnp.maximum(best, line)


SMEM = pl.BlockSpec(memory_space=pltpu.SMEM)
VMEM = pl.BlockSpec(memory_space=pltpu.VMEM)


def sized(*shape, dtype=jnp.float32):
    return jax.ShapeDtypeStruct(shape, dtype)


def working(count, length):
    long, short = pltpu.VMEM((length, LANES), jnp.float32), pltpu.VMEM((count, LANES), jnp.float32)
    return [long, short, short, long, long, long, long]


def settings(flops):
    return dict(
        compiler_params=pltpu.CompilerParams(vmem_limit_bytes=16 << 20),
        cost_estimate=pl.CostEstimate(flops=flops, bytes_accessed=1 << 21, transcendentals=0),
    )


def prepare(info, near, head, tail):
    channels, count = near.shape
    window = head.shape[1]
    return pl.pallas_call(
        own_body,
        out_shape=sized(count, channels * window, dtype=jnp.bfloat16),
        in_specs=[SMEM, VMEM, VMEM, VMEM],
        out_specs=VMEM,
        scratch_shapes=working(count, count + window),
        **settings(count * channels * window * 100),
    )(info, near, head, tail)


def crossed(info, mine, other, head, tail):
    channels, count = other.shape
    window = head.shape[1]
    return pl.pallas_call(
        cross_body,
        out_shape=[sized(4, count // 4)] * 2 + [sized(count, count // 2)],
        in_specs=[SMEM] + [VMEM] * 4,
        out_specs=[VMEM] * 3,
        scratch_shapes=[
            *working(count, count + window),
            *[pltpu.VMEM((count, WIDTH * LANES), jnp.bfloat16)] * 2,
            pltpu.VMEM((count, count), jnp.float32),
            *[pltpu.VMEM((count // 2, WIDTH * LANES), jnp.bfloat16)] * 2,
        ],
        **settings(2 * count * count * channels * window),
    )(info, mine, other, head, tail)


def paired(info, mine, part, partial):
    count, depth = mine.shape
    return pl.pallas_call(
        pair_body,
        out_shape=sized(4, count // 4),
        in_specs=[SMEM] + [VMEM] * 3,
        out_specs=VMEM,
        scratch_shapes=[
            *[pltpu.VMEM((count // 2, WIDTH * LANES), jnp.bfloat16)] * 2,
            pltpu.VMEM((count, count // 2), jnp.float32),
        ],
        **settings(count * count * depth),
    )(info, mine, part, partial)


def on_device(blocks, chans, series, tail, excl):
    return profile(blocks, chans, series, tail, excl)


def profile(blocks, chans, series, tail, excl):
    count = series.shape[1]
    window = tail.shape[1] + 1
    block = lax.axis_index("tm")
    chan = lax.axis_index("chan")
    axes = ("tm", "chan")
    places = [(b, c) for b in range(blocks) for c in range(chans)]

    def shifted(value, reach):
        pairs = [
            ((b + reach(c)) * chans + c, b * chans + c)
            for b, c in places
            if 0 <= b + reach(c) < blocks
        ]
        return lax.ppermute(value, axes, pairs)

    def swapped(value):
        return lax.ppermute(value, "chan", [(c, chans - 1 - c) for c in range(chans)])

    shift = chans - chan
    flags = [block + shift < blocks, block == blocks - 1, block + shift == blocks - 1]
    info = jnp.stack([excl[0], chan, shift] + [flag.astype(jnp.int32) for flag in flags])
    spare = jnp.zeros((series.shape[0], 1), series.dtype)
    partner = swapped(series)
    ends = [(b, c) for b, c in places if b >= blocks - 1 - chans]
    pairs = [(b * chans + c, b * chans + chans - 1 - c) for b, c in ends]
    partner_tail = lax.ppermute(tail, axes, pairs)
    padded = lax.optimization_barrier(jnp.concatenate([series, tail, spare], axis=1))
    near = jnp.concatenate([padded[:, :count], partner], axis=0)
    partner_tail = jnp.concatenate([partner_tail, spare], axis=1)
    ending = jnp.concatenate([padded[:, count:], partner_tail], axis=0)
    other = shifted(near, lambda c: chans - c)
    head = shifted(near[:, :window], lambda c: 1)
    other_head = shifted(near[:, :window], lambda c: chans + 1 - c)
    mine = prepare(info, near, head, ending)
    away, part, partial = crossed(info, mine, other, other_head, ending)
    home = shifted(away, lambda c: c - chans)
    best = paired(info, mine, part, partial)
    best = jnp.minimum(best, jnp.where(block - shift >= 0, home, CEILING))
    return jnp.minimum(best, swapped(best)).reshape(count)


def solution(mesh):
    placed = (P("chan", "tm"), P("chan", None), P())
    run = functools.partial(on_device, mesh.shape["tm"], mesh.shape["chan"])
    return jax.shard_map(run, mesh=mesh, in_specs=placed, out_specs=P("tm"), check_vma=False)
```

```python
import functools
import math

import jax
import jax.numpy as jnp
from jax import lax
from jax.experimental import pallas as pl
from jax.experimental.pallas import tpu as pltpu
from jax.sharding import PartitionSpec as P


EPSILON = 1e-05
CEILING = 4.0
FLOOR = 1.0 - CEILING
LANES = 128
WIDTH = 16


def transposed(value, target):
    length = value.shape[1]
    half = LANES // 2
    ahead = pltpu.roll(value, length - half, 1)
    for start in range(0, length, LANES):
        stop = start + LANES
        both = jnp.concatenate([value[:, start:stop], ahead[:, start:stop]], axis=0)
        target[start:stop, :] = both.T


def statistics(value, sums, moments, mean, scale):
    channels = value.shape[0]
    count = mean.shape[0]
    half = count // 2
    window = value.shape[1] - count
    for start in range(0, half + window, LANES):
        stop = start + LANES
        both = jnp.concatenate([value[:, start:stop], value[:, half + start : half + stop]], axis=0)
        sums[0][start:stop, :] = both.T
    size = 1
    level = 0
    while size < window:
        rows = -(-(half + window - 2 * size) // 8) * 8
        old, new = sums[level % 2], sums[(level + 1) % 2]
        for start in range(0, rows, 64):
            stop = min(start + 64, rows)
            here = old[start:stop, :]
            there = old[start + size : stop + size, :]
            gap = here - there
            square = gap * gap
            if size > 1:
                past = moments[level % 2]
                square += 2.0 * (past[start:stop, :] + past[start + size : stop + size, :])
            new[start:stop, :] = here + there
            moments[(level + 1) % 2][start:stop, :] = square
        level += 1
        size *= 2
    lower = lax.broadcasted_iota(jnp.int32, (64, LANES), 1) < LANES // 2
    for start in range(0, half, 64):
        rows = slice(start, start + 64)
        center = sums[level % 2][rows, :] * (1.0 / window)
        spread = moments[level % 2][rows, :] * (1.0 / (window * window))
        factor = lax.rsqrt(spread + EPSILON) * (1.0 / math.sqrt(window * channels))
        for target, part in ((mean, center), (scale, factor)):
            other = pltpu.roll(part, LANES // 2, 1)
            target[rows, :] = jnp.where(lower, part, other)
            target[half + start : half + start + 64, :] = jnp.where(lower, other, part)


def contract(left, right):
    return lax.dot_general(
        left, right, (((1,), (1,)), ((), ())), preferred_element_type=jnp.float32
    )


def fill(samples, means, scales, zed, step, base):
    for start in range(0, means.shape[0], 16):
        mean = means[start : start + 16, :]
        scale = scales[start : start + 16, :]
        for inner in range(0, WIDTH, 2):
            parts = [
                (samples[pl.ds(step + (start + inner + side), 16), :] - mean) * scale
                for side in range(2)
            ]
            zed[start : start + 16, pl.ds(base + inner * LANES, 2 * LANES)] = (
                jnp.concatenate(parts, axis=1).astype(jnp.bfloat16)
            )


def block_of(index):
    return pl.multiple_of(index * (WIDTH * LANES), WIDTH * LANES)


def gap_of(shape, row_start, column_start):
    rows = lax.broadcasted_iota(jnp.int32, shape, 0) + row_start
    columns = lax.broadcasted_iota(jnp.int32, shape, 1) + column_start
    return rows - columns


def rows_best(value):
    best = value[:, :LANES]
    for start in range(LANES, value.shape[1], LANES):
        best = jnp.maximum(best, value[:, start : start + LANES])
    return jnp.max(best.T, axis=0, keepdims=True)


def own_body(
    info, near, head, tail, zed_out,
    samples, means, scales, sums_a, sums_b, moments_a, moments_b,
):
    last = jnp.where(info[4] > 0, tail[...], head[...])
    value = jnp.concatenate([near[...], last], axis=1)
    transposed(value, samples)
    statistics(value, (sums_a, sums_b), (moments_a, moments_b), means, scales)

    def build(index, carry):
        fill(samples, means, scales, zed_out, index * WIDTH, block_of(index))
        return carry

    lax.fori_loop(0, zed_out.shape[1] // (WIDTH * LANES), build, 0)


def staged(mine, stage, base, chan):
    quarter = mine.shape[0] // 4
    for place in range(2):
        start = pl.multiple_of((2 * place + chan) * quarter, quarter)
        stage[place * quarter : (place + 1) * quarter, :] = mine[
            pl.ds(start, quarter), pl.ds(base, WIDTH * LANES)
        ]


def cross_body(
    info, mine, other, head, tail, away_out, part_out, pair_out,
    samples, means, scales, sums_a, sums_b, moments_a, moments_b, zed_a, zed_b, cross,
    stage_a, stage_b,
):
    count = means.shape[0]
    quarter = count // 4
    limit, shift, valid = info[0], info[2], info[3]
    last = jnp.where(info[5] > 0, tail[...], head[...])
    value = jnp.concatenate([other[...], last], axis=1)
    transposed(value, samples)
    staged(mine, stage_a, block_of(0), info[1])
    product = contract(mine[:, pl.ds(block_of(0), WIDTH * LANES)], stage_a[...])
    pair_out[...] = product
    statistics(value, (sums_a, sums_b), (moments_a, moments_b), means, scales)
    zeds = (zed_a, zed_b)
    cross[...] = jnp.zeros_like(cross)
    fill(samples, means, scales, zed_a, 0, 0)

    def pair(index, carry):
        for slot in range(2):
            block = 2 * index + slot
            cross[...] += contract(
                zeds[slot][...], mine[:, pl.ds(block_of(block), WIDTH * LANES)]
            )
            fill(samples, means, scales, zeds[1 - slot], (block + 1) * WIDTH, 0)
        return carry

    lax.fori_loop(0, mine.shape[1] // (2 * WIDTH * LANES), pair, 0, unroll=True)
    far = jnp.where(
        (gap_of(cross.shape, shift * count, 0) >= limit) & (valid > 0), cross[...], FLOOR
    )
    columns = jnp.max(far, axis=0, keepdims=True)
    for index in range(4):
        rows = slice(index * quarter, (index + 1) * quarter)
        away_out[index : index + 1, :] = 1.0 - rows_best(far[rows, :])
        part_out[index : index + 1, :] = columns[:, rows]


def pair_body(info, mine, part, partial, own_out, stage_a, stage_b, pair):
    count = mine.shape[0]
    quarter = count // 4
    limit, chan = info[0], info[1]
    stages = (stage_a, stage_b)
    starts = [
        pl.multiple_of(chan * quarter, quarter),
        pl.multiple_of(2 * quarter + chan * quarter, quarter),
    ]
    blocks = mine.shape[1] // (WIDTH * LANES)
    for index, block in enumerate(range(1, blocks)):
        stage = stages[index % 2]
        staged(mine, stage, block_of(block), chan)
        value = contract(mine[:, pl.ds(block_of(block), WIDTH * LANES)], stage[...])
        pair[...] = (pair if index else partial)[...] + value
    near = []
    for index, start in enumerate(starts):
        value = pair[:, index * quarter : (index + 1) * quarter]
        near.append(jnp.where(jnp.abs(gap_of(value.shape, 0, start)) >= limit, value, FLOOR))
    lines = [jnp.max(value, axis=0, keepdims=True) for value in near]
    both = jnp.maximum(near[0], near[1])
    for index in range(4):
        best = rows_best(both[index * quarter : (index + 1) * quarter, :])
        best = jnp.maximum(best, part[index : index + 1, :])
        line = jnp.where(chan == index % 2, lines[index // 2], FLOOR)
        own_out[index : index + 1, :] = 1.0 - jnp.maximum(best, line)


SMEM = pl.BlockSpec(memory_space=pltpu.SMEM)
VMEM = pl.BlockSpec(memory_space=pltpu.VMEM)


def sized(*shape, dtype=jnp.float32):
    return jax.ShapeDtypeStruct(shape, dtype)


def working(count, length):
    long, short = pltpu.VMEM((length, LANES), jnp.float32), pltpu.VMEM((count, LANES), jnp.float32)
    return [long, short, short, long, long, long, long]


def settings(flops):
    return dict(
        compiler_params=pltpu.CompilerParams(vmem_limit_bytes=16 << 20),
        cost_estimate=pl.CostEstimate(flops=flops, bytes_accessed=1 << 21, transcendentals=0),
    )


def prepare(info, near, head, tail):
    channels, count = near.shape
    window = head.shape[1]
    return pl.pallas_call(
        own_body,
        out_shape=sized(count, channels * window, dtype=jnp.bfloat16),
        in_specs=[SMEM, VMEM, VMEM, VMEM],
        out_specs=VMEM,
        scratch_shapes=working(count, count + window),
        **settings(count * channels * window * 100),
    )(info, near, head, tail)


def crossed(info, mine, other, head, tail):
    channels, count = other.shape
    window = head.shape[1]
    return pl.pallas_call(
        cross_body,
        out_shape=[sized(4, count // 4)] * 2 + [sized(count, count // 2)],
        in_specs=[SMEM] + [VMEM] * 4,
        out_specs=[VMEM] * 3,
        scratch_shapes=[
            *working(count, count + window),
            *[pltpu.VMEM((count, WIDTH * LANES), jnp.bfloat16)] * 2,
            pltpu.VMEM((count, count), jnp.float32),
            *[pltpu.VMEM((count // 2, WIDTH * LANES), jnp.bfloat16)] * 2,
        ],
        **settings(2 * count * count * channels * window),
    )(info, mine, other, head, tail)


def paired(info, mine, part, partial):
    count, depth = mine.shape
    return pl.pallas_call(
        pair_body,
        out_shape=sized(4, count // 4),
        in_specs=[SMEM] + [VMEM] * 3,
        out_specs=VMEM,
        scratch_shapes=[
            *[pltpu.VMEM((count // 2, WIDTH * LANES), jnp.bfloat16)] * 2,
            pltpu.VMEM((count, count // 2), jnp.float32),
        ],
        **settings(count * count * depth),
    )(info, mine, part, partial)


def on_device(blocks, chans, series, tail, excl):
    return profile(blocks, chans, series, tail, excl)


def profile(blocks, chans, series, tail, excl):
    count = series.shape[1]
    window = tail.shape[1] + 1
    block = lax.axis_index("tm")
    chan = lax.axis_index("chan")
    axes = ("tm", "chan")
    places = [(b, c) for b in range(blocks) for c in range(chans)]

    def shifted(value, reach):
        pairs = [
            ((b + reach(c)) * chans + c, b * chans + c)
            for b, c in places
            if 0 <= b + reach(c) < blocks
        ]
        return lax.ppermute(value, axes, pairs)

    def swapped(value):
        return lax.ppermute(value, "chan", [(c, chans - 1 - c) for c in range(chans)])

    shift = chans - chan
    flags = [block + shift < blocks, block == blocks - 1, block + shift == blocks - 1]
    info = jnp.stack([excl[0], chan, shift] + [flag.astype(jnp.int32) for flag in flags])
    spare = jnp.zeros((series.shape[0], 1), series.dtype)
    partner = swapped(series)
    ends = [(b, c) for b, c in places if b >= blocks - 1 - chans]
    pairs = [(b * chans + c, b * chans + chans - 1 - c) for b, c in ends]
    partner_tail = lax.ppermute(tail, axes, pairs)
    padded = lax.optimization_barrier(jnp.concatenate([series, tail, spare], axis=1))
    near = jnp.concatenate([padded[:, :count], partner], axis=0)
    partner_tail = jnp.concatenate([partner_tail, spare], axis=1)
    ending = jnp.concatenate([padded[:, count:], partner_tail], axis=0)
    other = shifted(near, lambda c: chans - c)
    head = shifted(near[:, :window], lambda c: 1)
    other_head = shifted(near[:, :window], lambda c: chans + 1 - c)
    mine = prepare(info, near, head, ending)
    away, part, partial = crossed(info, mine, other, other_head, ending)
    home = shifted(away, lambda c: c - chans)
    best = paired(info, mine, part, partial)
    best = jnp.minimum(best, jnp.where(block - shift >= 0, home, CEILING))
    return jnp.minimum(best, swapped(best)).reshape(count)


def solution(mesh):
    placed = (P("chan", "tm"), P("chan", None), P())
    run = functools.partial(on_device, mesh.shape["tm"], mesh.shape["chan"])
    return jax.shard_map(run, mesh=mesh, in_specs=placed, out_specs=P("tm"), check_vma=False)
```
